1024 devices in a mesh: dp: 64 (over z_lo, y, core), rep: 16 (over z_hi, x).
Axes of the slice: x: 4, y: 8, z: 16 (z_hi: 4, z_lo: 4; z = z_hi * 4 + z_lo), core: 2. Of those that a mesh axis runs over, the one named last changes fastest.
Arguments:
- clips: bfloat16 [1024, 1024, 256], P(('dp', 'rep')), may hold values from -6 to 6
- cotangent: bfloat16 [1024, 1024, 256], P(('dp', 'rep')), may hold values from -0.59765625 to 0.59765625
- alphas: float32 [2, 256], replicated, may hold values from 0.5 to 4
- weights: bfloat16 [524288], replicated, may hold values from -0.125 to 0.125
- master: float32 [524288], P('dp'), may hold values from -2 to 2
- first_moment: float32 [524288], P('dp'), may hold values from -6 to 6
- second_moment: float32 [524288], P('dp'), may hold values from 0.05 to 2
Outputs:
- new_weights: bfloat16 [524288], replicated
- new_master: float32 [524288], P('dp')
- new_first: float32 [524288], P('dp')
- new_second: float32 [524288], P('dp')
The draws below stay inside these ranges and needn't reach their ends.
All inputs are finite; a program needn't handle non-finite values.
Results may differ from the reference program's by a relative error of at most 0.0013.
Values may be sent and summed in bfloat16 or wider, within the bound.
No kernel may reach another device: no remote copies, remote signals or barrier semaphores. Data moves between devices by JAX's collectives and lax.ppermute only.
A program may use at most 32 MiB of HBM per device.

```python
import math
import jax
import jax.numpy as jnp
from jax import lax

CH = 256
TAPS = 7
DILATION = 3
FRAMES = 1024
CLIPS = 1024
PARAMS = 524288


def shard_levels(key, extent, shards, smallest, high):
    factor_of = 1.0
    for dim, shards_of in shards:
        steps = jax.random.uniform(jax.random.fold_in(jax.random.fold_in(key, 6), dim), (shards_of,), jnp.float32, smallest / len(shards), high / len(shards))
        factor_of = factor_of * jnp.repeat(jnp.exp(steps), extent[dim] // shards_of).reshape((-1,) + (1,) * (len(extent) - 1 - dim))
    return factor_of


def centred(rng, shape, scale, bound, shards=(), dtype=jnp.bfloat16):
    level = shard_levels(rng, shape, shards, -0.22, 0.18) if shards else 1.0
    entries = jax.random.normal(rng, shape, jnp.float32) * scale * level
    return jnp.minimum(jnp.maximum(entries, -bound), bound).astype(dtype)


def setup_inputs(seed: int = 0) -> dict:
    keys = jax.random.split(jax.random.key(seed), 8)
    clips = centred(keys[0], (CLIPS, FRAMES, CH), 1.0, 6.0, ((0, 1024),))
    cotangent = centred(keys[1], (CLIPS, FRAMES, CH), 0.1, 0.59765625, ((0, 1024),))
    alphas = jnp.clip(jnp.exp(jax.random.uniform(keys[2], (2, CH), jnp.float32, math.log(0.5), math.log(4.0))), 0.5, 4.0)
    weights = centred(keys[3], (PARAMS,), (TAPS * CH) ** -0.5, 0.125)
    master = centred(keys[4], (PARAMS,), 0.3, 2.0, ((0, 64),), jnp.float32)
    first_moment = centred(keys[5], (PARAMS,), 1.0, 6.0, ((0, 64),), jnp.float32)
    second_moment = jnp.clip(jnp.exp(math.log(2.0) - 3.6888794 * jax.random.uniform(keys[6], (PARAMS,), jnp.float32) ** shard_levels(keys[6], (PARAMS,), ((0, 64),), -0.2, 0.2)), 0.05, 2.0)
    return dict(clips=clips, cotangent=cotangent, alphas=alphas, weights=weights, master=master, first_moment=first_moment, second_moment=second_moment)


BIAS_ONE = 0.9999734386011124
BIAS_TWO = 0.09520785288629041

def snake(values, alpha):
    return values + jnp.sin(alpha * values) ** 2 / alpha

def clip_grads(clip, cot, alphas, weights):
    split = TAPS * CH * CH
    w_dilated = weights[:split].reshape(TAPS * CH, CH)
    w_point = weights[split:].reshape(CH, CH)
    first = snake(clip.astype(jnp.float32), alphas[0]).astype(jnp.bfloat16)
    reach = DILATION * (TAPS // 2)
    padded = jnp.pad(first, ((reach, reach), (0, 0)))
    windows = jnp.concatenate([padded[k * DILATION:k * DILATION + FRAMES] for k in range(TAPS)], axis=1)
    hidden = jnp.dot(windows, w_dilated, preferred_element_type=jnp.float32)
    second = snake(hidden, alphas[1]).astype(jnp.bfloat16)
    point_grad = jnp.dot(second.T, cot, preferred_element_type=jnp.float32)
    back = jnp.dot(cot, w_point.T, preferred_element_type=jnp.float32)
    d_hidden = (back * (1.0 + jnp.sin(2.0 * alphas[1] * hidden))).astype(jnp.bfloat16)
    dilated_grad = jnp.dot(windows.T, d_hidden, preferred_element_type=jnp.float32)
    return jnp.concatenate([dilated_grad.reshape(-1), point_grad.reshape(-1)])

def adam_update(gradient, master, first_moment, second_moment):
    new_first = 0.9 * first_moment + 0.1 * gradient
    new_second = 0.999 * second_moment + 0.001 * gradient * gradient
    new_master = master - 0.001 * (new_first / BIAS_ONE) / (jnp.sqrt(new_second / BIAS_TWO) + 1e-08)
    return (new_master, new_first, new_second)

def reference(clips, cotangent, alphas, weights, master, first_moment, second_moment):

    def accumulate(total, pair):
        return (total + clip_grads(pair[0], pair[1], alphas, weights), None)
    gradient, unused = lax.scan(accumulate, jnp.zeros((PARAMS,), jnp.float32), (clips, cotangent))
    new_master, new_first, new_second = adam_update(gradient, master, first_moment, second_moment)
    return (new_master.astype(jnp.bfloat16), new_master, new_first, new_second)
```

```python
import jax
import jax.numpy as jnp
from jax import lax
from jax.experimental import pallas as pl
from jax.experimental.pallas import tpu as pltpu
from jax.sharding import Mesh, PartitionSpec as P

CH = 256
TAPS = 7
DILATION = 3
PAD = 16
CHUNK = 256
BLOCK = 32

BIAS_ONE = 0.9999734386011124
BIAS_TWO = 0.09520785288629041

INV_PI = 0.3183098861837907
PI_A = 3.140625
PI_B = 9.67502593994140625e-4
PI_C = 1.509957990978376e-7


def reduced(t):
    n = jnp.round(t * INV_PI)
    return ((t - n * PI_A) - n * PI_B) - n * PI_C


def sine(r):
    z = r * r
    p = -2.4078282e-08
    for c in (2.75363800e-06, -1.98410853e-04, 8.33333284e-03, -1.66666672e-01):
        p = p * z + c
    return r + r * (z * p)


def cosine(r):
    z = r * r
    p = -2.62950522e-07
    for c in (2.47744738e-05, -1.38886506e-03, 4.16666605e-02, -0.5):
        p = p * z + c
    return 1.0 + z * p


def unit_kernel(core_ref, x_ref, cot_ref, al_ref, w_ref, keep_ref, send_ref, pad_ref, first_ref, second_ref):
    frames = x_ref.shape[0]
    even = core_ref[0] == 0
    a0 = al_ref[0:1, :]
    a1 = al_ref[1:2, :]
    r0 = 1.0 / a0
    r1 = 1.0 / a1
    pad_ref[0:PAD, :] = jnp.zeros((PAD, CH), jnp.float32)
    pad_ref[PAD + frames : 2 * PAD + frames, :] = jnp.zeros((PAD, CH), jnp.float32)
    for i in range(0, frames, CHUNK):
        x = x_ref[i : i + CHUNK, :].astype(jnp.float32)
        s = sine(reduced(a0 * x))
        first = (x + s * s * r0).astype(jnp.bfloat16)
        first_ref[i : i + CHUNK, :] = first
        pad_ref[PAD + i : PAD + i + CHUNK, :] = first.astype(jnp.float32)
    w_point = w_ref[TAPS * CH :, :]
    d_hidden = []
    for i in range(0, frames, CHUNK):
        hidden = None
        for k in range(TAPS):
            off = PAD + i + DILATION * (k - TAPS // 2)
            window = pad_ref[off : off + CHUNK, :].astype(jnp.bfloat16)
            part = jnp.dot(window, w_ref[k * CH : (k + 1) * CH, :], preferred_element_type=jnp.float32)
            hidden = part if hidden is None else hidden + part
        r = reduced(a1 * hidden)
        s = sine(r)
        second_ref[i : i + CHUNK, :] = (hidden + s * s * r1).astype(jnp.bfloat16)
        back = lax.dot_general(
            cot_ref[i : i + CHUNK, :], w_point, (((1,), (1,)), ((), ())), preferred_element_type=jnp.float32
        )
        d_hidden.append((back * (1.0 + 2.0 * s * cosine(r))).astype(jnp.bfloat16).astype(jnp.float32))
    for n, i in enumerate(range(0, frames, CHUNK)):
        pad_ref[PAD + i : PAD + i + CHUNK, :] = d_hidden[n]
    for k in range(TAPS + 1):
        if k < TAPS:
            off = PAD - DILATION * (k - TAPS // 2)
            left, right = first_ref[...], pad_ref[off : off + frames, :].astype(jnp.bfloat16)
        else:
            left, right = second_ref[...], cot_ref[...]
        grad = lax.dot_general(left, right, (((0,), (0,)), ((), ())), preferred_element_type=jnp.float32)
        for j in range(0, CH // BLOCK, 2):
            low = grad[j * BLOCK : (j + 1) * BLOCK, :]
            high = grad[(j + 1) * BLOCK : (j + 2) * BLOCK, :]
            slot = (k * (CH // BLOCK) + j) // 2
            place = (slot % 8) * 4 + slot // 8
            keep_ref[place] = jnp.where(even, low, high)
            send_ref[place] = jnp.where(even, high, low)


def clip_grads(clip, cot, alphas, weights, core):
    frames = clip.shape[0]
    vmem = pl.BlockSpec(memory_space=pltpu.VMEM)
    half = jax.ShapeDtypeStruct((32, BLOCK, CH), jnp.float32)
    return pl.pallas_call(
        unit_kernel,
        out_shape=(half, half),
        in_specs=[pl.BlockSpec(memory_space=pltpu.SMEM)] + [vmem] * 4,
        out_specs=(vmem, vmem),
        scratch_shapes=[
            pltpu.VMEM((frames + 2 * PAD, CH), jnp.float32),
            pltpu.VMEM((frames, CH), jnp.bfloat16),
            pltpu.VMEM((frames, CH), jnp.bfloat16),
        ],
        compiler_params=pltpu.CompilerParams(vmem_limit_bytes=40 << 20),
        cost_estimate=pl.CostEstimate(flops=2200000000, bytes_accessed=5 << 20, transcendentals=0),
    )(core, clip, cot, alphas, weights.reshape((TAPS + 1) * CH, CH))


def adam_update(gradient, master, first_moment, second_moment):
    new_first = 0.9 * first_moment + 0.1 * gradient
    new_second = 0.999 * second_moment + 0.001 * gradient * gradient
    new_master = master - 0.001 * (new_first / BIAS_ONE) / (jnp.sqrt(new_second / BIAS_TWO) + 1e-08)
    return (new_master, new_first, new_second)


SWAP = [(0, 1), (1, 0)]
CROSS = [(a * 4 + b, b * 4 + a) for a in range(4) for b in range(4)]


def shards(clips, cotangent, alphas, weights, master, first_moment, second_moment):
    core = lax.axis_index("c")
    there = lax.ppermute(jnp.stack([master, first_moment, second_moment]), ("zl", "x"), CROSS)
    keep, send = clip_grads(clips[0], cotangent[0], alphas, weights, core.reshape(1))
    part = keep + lax.ppermute(send, "c", SWAP)
    part = jnp.sum(lax.all_to_all(part, ("y", "x"), 0, 0, tiled=True), axis=0)
    for axis in ("zl", "zh"):
        part = jnp.broadcast_to(part[None], (4, BLOCK, CH))
        part = jnp.sum(lax.all_to_all(part, axis, 0, 0, tiled=True), axis=0)
    gradient = part.reshape(-1)
    mine = lax.ppermute(gradient, ("zl", "x"), CROSS)
    ahead, _, _ = adam_update(gradient, there[0], there[1], there[2])
    piece = ahead.astype(jnp.bfloat16).reshape(64, 128)
    piece = lax.all_to_all(jnp.broadcast_to(piece[None], (32, 64, 128)), ("y", "x"), 0, 0, tiled=True)
    other = lax.ppermute(piece, "c", SWAP)
    low = jnp.where(core == 0, piece, other)
    high = jnp.where(core == 0, other, piece)
    new_weights = jnp.stack([low, high], axis=1).reshape(8, 4, 2, 64, 128)
    new_weights = new_weights.transpose(1, 0, 2, 3, 4).reshape(-1)
    new_master, new_first, new_second = adam_update(mine, master, first_moment, second_moment)
    return (new_weights, new_master, new_first, new_second)


def solution(mesh):
    fine = Mesh(mesh.devices.reshape(4, 8, 2, 4, 4), ("zl", "y", "c", "zh", "x"))
    dp = ("zl", "y", "c")
    every = P(dp + ("zh", "x"), None, None)
    return jax.shard_map(
        shards,
        mesh=fine,
        in_specs=(every, every, P(), P(), P(dp), P(dp), P(dp)),
        out_specs=(P(), P(dp), P(dp), P(dp)),
        check_vma=False,
    )
```

```python
import jax
import jax.numpy as jnp
from jax import lax
from jax.experimental import pallas as pl
from jax.experimental.pallas import tpu as pltpu
from jax.sharding import Mesh, PartitionSpec as P

CH = 256
TAPS = 7
DILATION = 3
PAD = 16
CHUNK = 256
BLOCK = 32

BIAS_ONE = 0.9999734386011124
BIAS_TWO = 0.09520785288629041

INV_PI = 0.3183098861837907
PI_A = 3.140625
PI_B = 9.67502593994140625e-4
PI_C = 1.509957990978376e-7


def reduced(t):
    n = jnp.round(t * INV_PI)
    return ((t - n * PI_A) - n * PI_B) - n * PI_C


def sine(r):
    z = r * r
    p = -2.4078282e-08
    for c in (2.75363800e-06, -1.98410853e-04, 8.33333284e-03, -1.66666672e-01):
        p = p * z + c
    return r + r * (z * p)


def cosine(r):
    z = r * r
    p = -2.62950522e-07
    for c in (2.47744738e-05, -1.38886506e-03, 4.16666605e-02, -0.5):
        p = p * z + c
    return 1.0 + z * p


def unit_kernel(core_ref, x_ref, cot_ref, al_ref, w_ref, keep_ref, send_ref, pad_ref, first_ref, second_ref):
    frames = x_ref.shape[0]
    even = core_ref[0] == 0
    a0 = al_ref[0:1, :]
    a1 = al_ref[1:2, :]
    r0 = 1.0 / a0
    r1 = 1.0 / a1
    pad_ref[0:PAD, :] = jnp.zeros((PAD, CH), jnp.float32)
    pad_ref[PAD + frames : 2 * PAD + frames, :] = jnp.zeros((PAD, CH), jnp.float32)
    for i in range(0, frames, CHUNK):
        x = x_ref[i : i + CHUNK, :].astype(jnp.float32)
        s = sine(reduced(a0 * x))
        first = (x + s * s * r0).astype(jnp.bfloat16)
        first_ref[i : i + CHUNK, :] = first
        pad_ref[PAD + i : PAD + i + CHUNK, :] = first.astype(jnp.float32)
    w_point = w_ref[TAPS * CH :, :]
    d_hidden = []
    for i in range(0, frames, CHUNK):
        hidden = None
        for k in range(TAPS):
            off = PAD + i + DILATION * (k - TAPS // 2)
            window = pad_ref[off : off + CHUNK, :].astype(jnp.bfloat16)
            part = jnp.dot(window, w_ref[k * CH : (k + 1) * CH, :], preferred_element_type=jnp.float32)
            hidden = part if hidden is None else hidden + part
        r = reduced(a1 * hidden)
        s = sine(r)
        second_ref[i : i + CHUNK, :] = (hidden + s * s * r1).astype(jnp.bfloat16)
        back = lax.dot_general(
            cot_ref[i : i + CHUNK, :], w_point, (((1,), (1,)), ((), ())), preferred_element_type=jnp.float32
        )
        d_hidden.append((back * (1.0 + 2.0 * s * cosine(r))).astype(jnp.bfloat16).astype(jnp.float32))
    for n, i in enumerate(range(0, frames, CHUNK)):
        pad_ref[PAD + i : PAD + i + CHUNK, :] = d_hidden[n]
    for k in range(TAPS + 1):
        if k < TAPS:
            off = PAD - DILATION * (k - TAPS // 2)
            left, right = first_ref[...], pad_ref[off : off + frames, :].astype(jnp.bfloat16)
        else:
            left, right = second_ref[...], cot_ref[...]
        grad = lax.dot_general(left, right, (((0,), (0,)), ((), ())), preferred_element_type=jnp.float32)
        for j in range(0, CH // BLOCK, 2):
            low = grad[j * BLOCK : (j + 1) * BLOCK, :]
            high = grad[(j + 1) * BLOCK : (j + 2) * BLOCK, :]
            slot = (k * (CH // BLOCK) + j) // 2
            keep_ref[slot] = jnp.where(even, low, high)
            send_ref[slot] = jnp.where(even, high, low)


def clip_grads(clip, cot, alphas, weights, core):
    frames = clip.shape[0]
    vmem = pl.BlockSpec(memory_space=pltpu.VMEM)
    half = jax.ShapeDtypeStruct((32, BLOCK, CH), jnp.float32)
    return pl.pallas_call(
        unit_kernel,
        out_shape=(half, half),
        in_specs=[pl.BlockSpec(memory_space=pltpu.SMEM)] + [vmem] * 4,
        out_specs=(vmem, vmem),
        scratch_shapes=[
            pltpu.VMEM((frames + 2 * PAD, CH), jnp.float32),
            pltpu.VMEM((frames, CH), jnp.bfloat16),
            pltpu.VMEM((frames, CH), jnp.bfloat16),
        ],
        compiler_params=pltpu.CompilerParams(vmem_limit_bytes=40 << 20),
        cost_estimate=pl.CostEstimate(flops=2200000000, bytes_accessed=5 << 20, transcendentals=0),
    )(core, clip, cot, alphas, weights.reshape((TAPS + 1) * CH, CH))


def adam_update(gradient, master, first_moment, second_moment):
    new_first = 0.9 * first_moment + 0.1 * gradient
    new_second = 0.999 * second_moment + 0.001 * gradient * gradient
    new_master = master - 0.001 * (new_first / BIAS_ONE) / (jnp.sqrt(new_second / BIAS_TWO) + 1e-08)
    return (new_master, new_first, new_second)


SWAP = [(0, 1), (1, 0)]


def packed(values):
    root = jnp.sqrt(jnp.abs(values))
    return jnp.where(values < 0, -root, root).astype(jnp.float16)


def unpacked(roots):
    roots = roots.astype(jnp.float32)
    return roots * jnp.abs(roots)


def shards(clips, cotangent, alphas, weights, master, first_moment, second_moment):
    core = lax.axis_index("c")
    keep, send = clip_grads(clips[0], cotangent[0], alphas, weights, core.reshape(1))
    part = packed(keep + lax.ppermute(send, "c", SWAP))
    part = lax.all_to_all(part.reshape(128, BLOCK // 4, CH), ("zl", "y", "x"), 0, 0, tiled=True)
    part = jnp.broadcast_to(jnp.sum(unpacked(part), axis=0)[None], (16, BLOCK // 4, CH))
    part = lax.all_to_all(part, ("zh", "x"), 0, 0, tiled=True)
    gradient = jnp.sum(part.reshape(4, BLOCK, CH), axis=0).reshape(-1)
    new_master, new_first, new_second = adam_update(gradient, master, first_moment, second_moment)
    piece = new_master.astype(jnp.bfloat16).reshape(64, 128)
    piece = lax.all_to_all(jnp.broadcast_to(piece[None], (32, 64, 128)), ("zl", "y"), 0, 0, tiled=True)
    other = lax.ppermute(piece, "c", SWAP)
    place = lax.broadcasted_iota(jnp.int32, (32, 2, 64, 128), 1)
    new_weights = jnp.where(place == core, piece[:, None], other[:, None]).reshape(-1)
    return (new_weights, new_master, new_first, new_second)


def solution(mesh):
    fine = Mesh(mesh.devices.reshape(4, 8, 2, 4, 4), ("zl", "y", "c", "zh", "x"))
    dp = ("zl", "y", "c")
    every = P(dp + ("zh", "x"), None, None)
    return jax.shard_map(
        shards,
        mesh=fine,
        in_specs=(every, every, P(), P(), P(dp), P(dp), P(dp)),
        out_specs=(P(), P(dp), P(dp), P(dp)),
        check_vma=False,
    )
```

```python
import jax
import jax.numpy as jnp
from jax import lax
from jax.experimental import pallas as pl
from jax.experimental.pallas import tpu as pltpu
from jax.sharding import Mesh, PartitionSpec as P

CH = 256
TAPS = 7
DILATION = 3
PAD = 16
CHUNK = 256
BLOCK = 32
QUARTER = BLOCK // 4

BIAS_ONE = 0.9999734386011124
BIAS_TWO = 0.09520785288629041

INV_PI = 0.3183098861837907
PI_A = 3.140625
PI_B = 9.67502593994140625e-4
PI_C = 1.509957990978376e-7


def reduced(t):
    n = jnp.round(t * INV_PI)
    return ((t - n * PI_A) - n * PI_B) - n * PI_C


def sine(r):
    z = r * r
    p = -2.4078282e-08
    for c in (2.75363800e-06, -1.98410853e-04, 8.33333284e-03, -1.66666672e-01):
        p = p * z + c
    return r + r * (z * p)


def cosine(r):
    z = r * r
    p = -2.62950522e-07
    for c in (2.47744738e-05, -1.38886506e-03, 4.16666605e-02, -0.5):
        p = p * z + c
    return 1.0 + z * p


def unit_kernel(
    core_ref, x_hbm, cot_hbm, al_hbm, w_hbm, keep_ref, send_ref,
    x_ref, cot_ref, al_ref, flat_ref, wide_ref, w_ref, pad_ref, first_ref, second_ref, sems,
):
    copies = [
        pltpu.make_async_copy(source, target, sems.at[n])
        for n, (source, target) in enumerate(
            ((al_hbm, al_ref), (x_hbm, x_ref), (w_hbm, flat_ref), (cot_hbm, cot_ref))
        )
    ]
    for copy in copies:
        copy.start()
    frames = x_ref.shape[0]
    rows = w_ref.shape[0]
    even = core_ref[0] == 0
    pad_ref[0:PAD, :] = jnp.zeros((PAD, CH), jnp.float32)
    pad_ref[PAD + frames : 2 * PAD + frames, :] = jnp.zeros((PAD, CH), jnp.float32)
    copies[0].wait()
    a0 = al_ref[0:1, :]
    a1 = al_ref[1:2, :]
    r0 = 1.0 / a0
    r1 = 1.0 / a1
    copies[1].wait()
    for i in range(0, frames, CHUNK):
        x = x_ref[i : i + CHUNK, :].astype(jnp.float32)
        s = sine(reduced(a0 * x))
        first = (x + s * s * r0).astype(jnp.bfloat16)
        first_ref[i : i + CHUNK, :] = first
        pad_ref[PAD + i : PAD + i + CHUNK, :] = first.astype(jnp.float32)
    copies[2].wait()
    wide_ref[...] = flat_ref[...].astype(jnp.float32)
    for side in range(2):
        half = wide_ref[pl.ds(side, rows, stride=2), :]
        w_ref[:, side * 128 : (side + 1) * 128] = half.astype(jnp.bfloat16)
    w_point = w_ref[TAPS * CH :, :]
    copies[3].wait()
    d_hidden = []
    for i in range(0, frames, CHUNK):
        hidden = None
        for k in range(TAPS):
            off = PAD + i + DILATION * (k - TAPS // 2)
            window = pad_ref[off : off + CHUNK, :].astype(jnp.bfloat16)
            part = jnp.dot(window, w_ref[k * CH : (k + 1) * CH, :], preferred_element_type=jnp.float32)
            hidden = part if hidden is None else hidden + part
        r = reduced(a1 * hidden)
        s = sine(r)
        second_ref[i : i + CHUNK, :] = (hidden + s * s * r1).astype(jnp.bfloat16)
        back = lax.dot_general(
            cot_ref[i : i + CHUNK, :], w_point, (((1,), (1,)), ((), ())), preferred_element_type=jnp.float32
        )
        d_hidden.append((back * (1.0 + 2.0 * s * cosine(r))).astype(jnp.bfloat16).astype(jnp.float32))
    for n, i in enumerate(range(0, frames, CHUNK)):
        pad_ref[PAD + i : PAD + i + CHUNK, :] = d_hidden[n]
    for k in range(TAPS + 1):
        if k < TAPS:
            off = PAD - DILATION * (k - TAPS // 2)
            left, right = first_ref[...], pad_ref[off : off + frames, :].astype(jnp.bfloat16)
        else:
            left, right = second_ref[...], cot_ref[...]
        grad = lax.dot_general(left, right, (((0,), (0,)), ((), ())), preferred_element_type=jnp.float32)
        for j in range(0, CH // BLOCK, 2):
            slot = (k * (CH // BLOCK) + j) // 2
            for q in range(4):
                row = j * BLOCK + q * QUARTER
                low = grad[row : row + QUARTER, :]
                high = grad[row + BLOCK : row + BLOCK + QUARTER, :]
                place = (slot % 8) * 4 + q, pl.ds(slot // 8 * QUARTER, QUARTER)
                keep_ref[place] = jnp.where(even, low, high)
                send_ref[place] = jnp.where(even, high, low)


def clip_grads(clip, cot, alphas, weights, core):
    frames = clip.shape[0]
    rows = (TAPS + 1) * CH
    vmem = pl.BlockSpec(memory_space=pltpu.VMEM)
    half = jax.ShapeDtypeStruct((32, 4 * QUARTER, CH), jnp.float32)
    return pl.pallas_call(
        unit_kernel,
        out_shape=(half, half),
        in_specs=[pl.BlockSpec(memory_space=pltpu.SMEM)] + [pl.BlockSpec(memory_space=pltpu.HBM)] * 4,
        out_specs=(vmem, vmem),
        scratch_shapes=[
            pltpu.VMEM((frames, CH), jnp.bfloat16),
            pltpu.VMEM((frames, CH), jnp.bfloat16),
            pltpu.VMEM((2, CH), jnp.float32),
            pltpu.VMEM((2 * rows, 128), jnp.bfloat16),
            pltpu.VMEM((2 * rows, 128), jnp.float32),
            pltpu.VMEM((rows, CH), jnp.bfloat16),
            pltpu.VMEM((frames + 2 * PAD, CH), jnp.float32),
            pltpu.VMEM((frames, CH), jnp.bfloat16),
            pltpu.VMEM((frames, CH), jnp.bfloat16),
            pltpu.SemaphoreType.DMA((4,)),
        ],
        compiler_params=pltpu.CompilerParams(vmem_limit_bytes=40 << 20),
        cost_estimate=pl.CostEstimate(flops=2200000000, bytes_accessed=5 << 20, transcendentals=0),
    )(core, *[pltpu.with_memory_space_constraint(v, pltpu.HBM) for v in (clip, cot, alphas, weights.reshape(2 * rows, 128))])


def adam_update(gradient, master, first_part, second_part):
    new_first = first_part + 0.1 * gradient
    new_second = second_part + 0.001 * gradient * gradient
    new_master = master - 0.001 * (new_first / BIAS_ONE) / (jnp.sqrt(new_second / BIAS_TWO) + 1e-08)
    return (new_master, new_first, new_second)


SWAP = [(0, 1), (1, 0)]


def packed(values):
    root = jnp.sqrt(jnp.abs(values))
    return jnp.where(values < 0, -root, root).astype(jnp.float16)


def unpacked(roots):
    roots = roots.astype(jnp.float32)
    return roots * jnp.abs(roots)


def shards(clips, cotangent, alphas, weights, master, first_moment, second_moment):
    core = lax.axis_index("c")
    keep, send = clip_grads(clips[0], cotangent[0], alphas, weights, core.reshape(1))
    ready = jnp.concatenate([master, 0.9 * first_moment, 0.999 * second_moment])
    recv, ready = lax.optimization_barrier((lax.ppermute(send, "c", SWAP), ready))
    part = lax.all_to_all(packed(keep + recv), ("y", "x"), 0, 0, tiled=True)
    part = jnp.sum(unpacked(part), axis=0).reshape(4, QUARTER, CH)
    part = jnp.sum(lax.all_to_all(part, "zl", 0, 0, tiled=True), axis=0)
    part = jnp.broadcast_to(part[None], (16, QUARTER, CH))
    part = lax.all_to_all(part, ("zh", "x"), 0, 0, tiled=True)
    gradient = jnp.sum(part.reshape(4, BLOCK, CH), axis=0).reshape(-1)
    new_master, new_first, new_second = adam_update(gradient, *jnp.split(ready, 3))
    piece = new_master.astype(jnp.bfloat16).reshape(64, 128)
    piece = lax.all_to_all(jnp.broadcast_to(piece[None], (32, 64, 128)), ("zl", "y"), 0, 0, tiled=True)
    other = lax.ppermute(piece, "c", SWAP)
    place = lax.broadcasted_iota(jnp.int32, (32, 2, 64, 128), 1)
    new_weights = jnp.where(place == core, piece[:, None], other[:, None]).reshape(-1)
    return (new_weights, new_master, new_first, new_second)


def solution(mesh):
    fine = Mesh(mesh.devices.reshape(4, 8, 2, 4, 4), ("zl", "y", "c", "zh", "x"))
    dp = ("zl", "y", "c")
    every = P(dp + ("zh", "x"), None, None)
    return jax.shard_map(
        shards,
        mesh=fine,
        in_specs=(every, every, P(), P(), P(dp), P(dp), P(dp)),
        out_specs=(P(), P(dp), P(dp), P(dp)),
        check_vma=False,
    )
```

```python
import jax
import jax.numpy as jnp
from jax import lax
from jax.experimental import pallas as pl
from jax.experimental.pallas import tpu as pltpu
from jax.sharding import Mesh, PartitionSpec as P

CH = 256
TAPS = 7
DILATION = 3
PAD = 16
CHUNK = 256
BLOCK = 32
QUARTER = BLOCK // 4

BIAS_ONE = 0.9999734386011124
BIAS_TWO = 0.09520785288629041

INV_PI = 0.3183098861837907
PI_A = 3.140625
PI_B = 9.67502593994140625e-4
PI_C = 1.509957990978376e-7


def reduced(t):
    n = jnp.round(t * INV_PI)
    return ((t - n * PI_A) - n * PI_B) - n * PI_C


def sine(r):
    z = r * r
    p = -2.4078282e-08
    for c in (2.75363800e-06, -1.98410853e-04, 8.33333284e-03, -1.66666672e-01):
        p = p * z + c
    return r + r * (z * p)


def cosine(r):
    z = r * r
    p = -2.62950522e-07
    for c in (2.47744738e-05, -1.38886506e-03, 4.16666605e-02, -0.5):
        p = p * z + c
    return 1.0 + z * p


def unit_kernel(
    core_ref, x_hbm, cot_hbm, al_hbm, w_hbm, keep_ref, send_ref,
    x_ref, cot_ref, al_ref, flat_ref, wide_ref, w_ref, pad_ref, first_ref, second_ref, sems,
):
    copies = [
        pltpu.make_async_copy(source, target, sems.at[n])
        for n, (source, target) in enumerate(
            ((al_hbm, al_ref), (x_hbm, x_ref), (w_hbm, flat_ref), (cot_hbm, cot_ref))
        )
    ]
    for copy in copies:
        copy.start()
    frames = x_ref.shape[0]
    rows = w_ref.shape[0]
    even = core_ref[0] == 0
    pad_ref[0:PAD, :] = jnp.zeros((PAD, CH), jnp.float32)
    pad_ref[PAD + frames : 2 * PAD + frames, :] = jnp.zeros((PAD, CH), jnp.float32)
    copies[0].wait()
    a0 = al_ref[0:1, :]
    a1 = al_ref[1:2, :]
    r0 = 1.0 / a0
    r1 = 1.0 / a1
    copies[1].wait()
    for i in range(0, frames, CHUNK):
        x = x_ref[i : i + CHUNK, :].astype(jnp.float32)
        s = sine(reduced(a0 * x))
        first = (x + s * s * r0).astype(jnp.bfloat16)
        first_ref[i : i + CHUNK, :] = first
        pad_ref[PAD + i : PAD + i + CHUNK, :] = first.astype(jnp.float32)
    copies[2].wait()
    wide_ref[...] = flat_ref[...].astype(jnp.float32)
    for side in range(2):
        half = wide_ref[pl.ds(side, rows, stride=2), :]
        w_ref[:, side * 128 : (side + 1) * 128] = half.astype(jnp.bfloat16)
    w_point = w_ref[TAPS * CH :, :]
    copies[3].wait()
    d_hidden = []
    for i in range(0, frames, CHUNK):
        hidden = None
        for k in range(TAPS):
            off = PAD + i + DILATION * (k - TAPS // 2)
            window = pad_ref[off : off + CHUNK, :].astype(jnp.bfloat16)
            part = jnp.dot(window, w_ref[k * CH : (k + 1) * CH, :], preferred_element_type=jnp.float32)
            hidden = part if hidden is None else hidden + part
        r = reduced(a1 * hidden)
        s = sine(r)
        second_ref[i : i + CHUNK, :] = (hidden + s * s * r1).astype(jnp.bfloat16)
        back = lax.dot_general(
            cot_ref[i : i + CHUNK, :], w_point, (((1,), (1,)), ((), ())), preferred_element_type=jnp.float32
        )
        d_hidden.append((back * (1.0 + 2.0 * s * cosine(r))).astype(jnp.bfloat16).astype(jnp.float32))
    for n, i in enumerate(range(0, frames, CHUNK)):
        pad_ref[PAD + i : PAD + i + CHUNK, :] = d_hidden[n]
    for k in range(TAPS + 1):
        if k < TAPS:
            off = PAD - DILATION * (k - TAPS // 2)
            left, right = first_ref[...], pad_ref[off : off + frames, :].astype(jnp.bfloat16)
        else:
            left, right = second_ref[...], cot_ref[...]
        grad = lax.dot_general(left, right, (((0,), (0,)), ((), ())), preferred_element_type=jnp.float32)
        for j in range(0, CH // BLOCK, 2):
            low = grad[j * BLOCK : (j + 1) * BLOCK, :]
            high = grad[(j + 1) * BLOCK : (j + 2) * BLOCK, :]
            slot = (k * (CH // BLOCK) + j) // 2
            keep_ref[slot] = jnp.where(even, low, high)
            send_ref[slot] = jnp.where(even, high, low)


def clip_grads(clip, cot, alphas, weights, core):
    frames = clip.shape[0]
    rows = (TAPS + 1) * CH
    vmem = pl.BlockSpec(memory_space=pltpu.VMEM)
    half = jax.ShapeDtypeStruct((32, BLOCK, CH), jnp.float32)
    return pl.pallas_call(
        unit_kernel,
        out_shape=(half, half),
        in_specs=[pl.BlockSpec(memory_space=pltpu.SMEM)] + [pl.BlockSpec(memory_space=pltpu.HBM)] * 4,
        out_specs=(vmem, vmem),
        scratch_shapes=[
            pltpu.VMEM((frames, CH), jnp.bfloat16),
            pltpu.VMEM((frames, CH), jnp.bfloat16),
            pltpu.VMEM((2, CH), jnp.float32),
            pltpu.VMEM((2 * rows, 128), jnp.bfloat16),
            pltpu.VMEM((2 * rows, 128), jnp.float32),
            pltpu.VMEM((rows, CH), jnp.bfloat16),
            pltpu.VMEM((frames + 2 * PAD, CH), jnp.float32),
            pltpu.VMEM((frames, CH), jnp.bfloat16),
            pltpu.VMEM((frames, CH), jnp.bfloat16),
            pltpu.SemaphoreType.DMA((4,)),
        ],
        compiler_params=pltpu.CompilerParams(vmem_limit_bytes=40 << 20),
        cost_estimate=pl.CostEstimate(flops=2200000000, bytes_accessed=5 << 20, transcendentals=0),
    )(core, *[pltpu.with_memory_space_constraint(v, pltpu.HBM) for v in (clip, cot, alphas, weights.reshape(2 * rows, 128))])


def adam_update(gradient, master, first_part, second_part):
    new_first = first_part + 0.1 * gradient
    new_second = second_part + 0.001 * gradient * gradient
    new_master = master - 0.001 * (new_first / BIAS_ONE) / (jnp.sqrt(new_second / BIAS_TWO) + 1e-08)
    return (new_master, new_first, new_second)


SWAP = [(0, 1), (1, 0)]


def packed(values):
    root = jnp.sqrt(jnp.abs(values))
    return jnp.where(values < 0, -root, root).astype(jnp.float16)


def unpacked(roots):
    roots = roots.astype(jnp.float32)
    return roots * jnp.abs(roots)


def shards(clips, cotangent, alphas, weights, master, first_moment, second_moment):
    core = lax.axis_index("c")
    keep, send = clip_grads(clips[0], cotangent[0], alphas, weights, core.reshape(1))
    ready = jnp.concatenate([master, 0.9 * first_moment, 0.999 * second_moment])
    recv, ready = lax.optimization_barrier((lax.ppermute(send, "c", SWAP), ready))
    part = packed(keep + recv).reshape(128, QUARTER, CH)
    part = jnp.sum(unpacked(lax.all_to_all(part, ("zl", "y", "x"), 0, 0, tiled=True)), axis=0)
    part = jnp.broadcast_to(part[None], (16, QUARTER, CH))
    part = lax.all_to_all(part, ("zh", "x"), 0, 0, tiled=True)
    gradient = jnp.sum(part.reshape(4, BLOCK, CH), axis=0).reshape(-1)
    new_master, new_first, new_second = adam_update(gradient, *jnp.split(ready, 3))
    piece = new_master.astype(jnp.bfloat16).reshape(64, 128)
    piece = lax.all_to_all(jnp.broadcast_to(piece[None], (32, 64, 128)), ("zl", "y"), 0, 0, tiled=True)
    other = lax.ppermute(piece, "c", SWAP)
    place = lax.broadcasted_iota(jnp.int32, (32, 2, 64, 128), 1)
    new_weights = jnp.where(place == core, piece[:, None], other[:, None]).reshape(-1)
    return (new_weights, new_master, new_first, new_second)


def solution(mesh):
    fine = Mesh(mesh.devices.reshape(4, 8, 2, 4, 4), ("zl", "y", "c", "zh", "x"))
    dp = ("zl", "y", "c")
    every = P(dp + ("zh", "x"), None, None)
    return jax.shard_map(
        shards,
        mesh=fine,
        in_specs=(every, every, P(), P(), P(dp), P(dp), P(dp)),
        out_specs=(P(), P(dp), P(dp), P(dp)),
        check_vma=False,
    )
```

```python
import jax
import jax.numpy as jnp
from jax import lax
from jax.experimental import pallas as pl
from jax.experimental.pallas import tpu as pltpu
from jax.sharding import Mesh, PartitionSpec as P

CH = 256
TAPS = 7
DILATION = 3
PAD = 16
CHUNK = 256
BLOCK = 32
QUARTER = BLOCK // 4

BIAS_ONE = 0.9999734386011124
BIAS_TWO = 0.09520785288629041

INV_PI = 0.3183098861837907


def turned(halves):
    return halves - jnp.round(halves)


def sine(u, z):
    p = 0.07764279097318649
    for c in (-0.5982846617698669, 2.550076723098755, -5.167709827423096, 3.1415927410125732):
        p = p * z + c
    return u * p


def double_cosine(z):
    p = -0.04924729838967323
    for c in (0.47014570236206055, -2.6704795360565186, 8.117423057556152, -9.869604110717773, 2.0):
        p = p * z + c
    return p


def unit_kernel(
    core_ref, x_hbm, cot_hbm, al_hbm, w_hbm, keep_ref, send_ref,
    x_ref, cot_ref, al_ref, flat_ref, wide_ref, w_ref, pad_ref, first_ref, second_ref, windows_ref, sems,
):
    copies = [
        pltpu.make_async_copy(source, target, sems.at[n])
        for n, (source, target) in enumerate(
            ((al_hbm, al_ref), (x_hbm, x_ref), (w_hbm, flat_ref), (cot_hbm, cot_ref))
        )
    ]
    for copy in copies:
        copy.start()
    frames = x_ref.shape[0]
    rows = w_ref.shape[0]
    even = core_ref[0] == 0
    pad_ref[0:PAD, :] = jnp.zeros((PAD, CH), jnp.bfloat16)
    pad_ref[PAD + frames : 2 * PAD + frames, :] = jnp.zeros((PAD, CH), jnp.bfloat16)
    copies[0].wait()
    a0 = al_ref[0:1, :]
    a1 = al_ref[1:2, :]
    r0 = 1.0 / a0
    r1 = 1.0 / a1
    t0 = a0 * INV_PI
    t1 = a1 * INV_PI
    copies[1].wait()
    for i in range(0, frames, CHUNK):
        x = x_ref[i : i + CHUNK, :].astype(jnp.float32)
        u = turned(t0 * x)
        s = sine(u, u * u)
        first = (x + s * s * r0).astype(jnp.bfloat16)
        first_ref[i : i + CHUNK, :] = first
        pad_ref[PAD + i : PAD + i + CHUNK, :] = first
    copies[2].wait()
    wide_ref[...] = flat_ref[...].astype(jnp.float32)
    for side in range(2):
        half = wide_ref[pl.ds(side, rows, stride=2), :]
        w_ref[:, side * 128 : (side + 1) * 128] = half.astype(jnp.bfloat16)
    w_point = w_ref[TAPS * CH :, :]
    copies[3].wait()
    for k in range(TAPS):
        off = PAD + DILATION * (k - TAPS // 2)
        windows_ref[:, k * CH : (k + 1) * CH] = pad_ref[off : off + frames, :]
    d_hidden = []
    for i in range(0, frames, CHUNK):
        hidden = jnp.dot(windows_ref[i : i + CHUNK, :], w_ref[: TAPS * CH, :], preferred_element_type=jnp.float32)
        u = turned(t1 * hidden)
        z = u * u
        s = sine(u, z)
        second_ref[i : i + CHUNK, :] = (hidden + s * s * r1).astype(jnp.bfloat16)
        back = lax.dot_general(
            cot_ref[i : i + CHUNK, :], w_point, (((1,), (1,)), ((), ())), preferred_element_type=jnp.float32
        )
        d_hidden.append((back * (1.0 + s * double_cosine(z))).astype(jnp.bfloat16))
    for n, i in enumerate(range(0, frames, CHUNK)):
        pad_ref[PAD + i : PAD + i + CHUNK, :] = d_hidden[n]
    for k in range(TAPS + 1):
        if k < TAPS:
            off = PAD - DILATION * (k - TAPS // 2)
            left, right = first_ref[...], pad_ref[off : off + frames, :]
        else:
            left, right = second_ref[...], cot_ref[...]
        grad = lax.dot_general(left, right, (((0,), (0,)), ((), ())), preferred_element_type=jnp.float32)
        for j in range(0, CH // BLOCK, 2):
            low = grad[j * BLOCK : (j + 1) * BLOCK, :]
            high = grad[(j + 1) * BLOCK : (j + 2) * BLOCK, :]
            slot = (k * (CH // BLOCK) + j) // 2
            keep_ref[slot] = jnp.where(even, low, high)
            send_ref[slot] = jnp.where(even, high, low)


def clip_grads(clip, cot, alphas, weights, core):
    frames = clip.shape[0]
    rows = (TAPS + 1) * CH
    vmem = pl.BlockSpec(memory_space=pltpu.VMEM)
    half = jax.ShapeDtypeStruct((32, BLOCK, CH), jnp.float32)
    return pl.pallas_call(
        unit_kernel,
        out_shape=(half, half),
        in_specs=[pl.BlockSpec(memory_space=pltpu.SMEM)] + [pl.BlockSpec(memory_space=pltpu.HBM)] * 4,
        out_specs=(vmem, vmem),
        scratch_shapes=[
            pltpu.VMEM((frames, CH), jnp.bfloat16),
            pltpu.VMEM((frames, CH), jnp.bfloat16),
            pltpu.VMEM((2, CH), jnp.float32),
            pltpu.VMEM((2 * rows, 128), jnp.bfloat16),
            pltpu.VMEM((2 * rows, 128), jnp.float32),
            pltpu.VMEM((rows, CH), jnp.bfloat16),
            pltpu.VMEM((frames + 2 * PAD, CH), jnp.bfloat16),
            pltpu.VMEM((frames, CH), jnp.bfloat16),
            pltpu.VMEM((frames, CH), jnp.bfloat16),
            pltpu.VMEM((frames, TAPS * CH), jnp.bfloat16),
            pltpu.SemaphoreType.DMA((4,)),
        ],
        compiler_params=pltpu.CompilerParams(vmem_limit_bytes=40 << 20),
        cost_estimate=pl.CostEstimate(flops=2200000000, bytes_accessed=5 << 20, transcendentals=0),
    )(core, *[pltpu.with_memory_space_constraint(v, pltpu.HBM) for v in (clip, cot, alphas, weights.reshape(2 * rows, 128))])


def adam_update(gradient, master, first_part, second_part):
    new_first = first_part + 0.1 * gradient
    new_second = second_part + 0.001 * gradient * gradient
    new_master = master - 0.001 * (new_first / BIAS_ONE) / (jnp.sqrt(new_second / BIAS_TWO) + 1e-08)
    return (new_master, new_first, new_second)


SWAP = [(0, 1), (1, 0)]


def packed(values):
    root = jnp.sqrt(jnp.abs(values))
    return jnp.where(values < 0, -root, root).astype(jnp.float16)


def unpacked(roots):
    roots = roots.astype(jnp.float32)
    return roots * jnp.abs(roots)


def shards(clips, cotangent, alphas, weights, master, first_moment, second_moment):
    core = lax.axis_index("c")
    keep, send = clip_grads(clips[0], cotangent[0], alphas, weights, core.reshape(1))
    ready = jnp.concatenate([master, 0.9 * first_moment, 0.999 * second_moment])
    recv, ready = lax.optimization_barrier((lax.ppermute(send, "c", SWAP), ready))
    part = packed(keep + recv).reshape(128, QUARTER, CH)
    part = jnp.sum(unpacked(lax.all_to_all(part, ("zl", "y", "x"), 0, 0, tiled=True)), axis=0)
    part = jnp.broadcast_to(part[None], (16, QUARTER, CH))
    part = lax.all_to_all(part, ("zh", "x"), 0, 0, tiled=True)
    gradient = jnp.sum(part.reshape(4, BLOCK, CH), axis=0).reshape(-1)
    new_master, new_first, new_second = adam_update(gradient, *jnp.split(ready, 3))
    piece = new_master.astype(jnp.bfloat16).reshape(64, 128)
    piece = lax.all_to_all(jnp.broadcast_to(piece[None], (32, 64, 128)), ("zl", "y"), 0, 0, tiled=True)
    other = lax.ppermute(piece, "c", SWAP)
    place = lax.broadcasted_iota(jnp.int32, (32, 2, 64, 128), 1)
    new_weights = jnp.where(place == core, piece[:, None], other[:, None]).reshape(-1)
    return (new_weights, new_master, new_first, new_second)


def solution(mesh):
    fine = Mesh(mesh.devices.reshape(4, 8, 2, 4, 4), ("zl", "y", "c", "zh", "x"))
    dp = ("zl", "y", "c")
    every = P(dp + ("zh", "x"), None, None)
    return jax.shard_map(
        shards,
        mesh=fine,
        in_specs=(every, every, P(), P(), P(dp), P(dp), P(dp)),
        out_specs=(P(), P(dp), P(dp), P(dp)),
        check_vma=False,
    )
```

```python
import jax
import jax.numpy as jnp
from jax import lax
from jax.experimental import pallas as pl
from jax.experimental.pallas import tpu as pltpu
from jax.sharding import Mesh, PartitionSpec as P

CH = 256
TAPS = 7
DILATION = 3
PAD = 16
CHUNK = 256
BLOCK = 32
QUARTER = BLOCK // 4

BIAS_ONE = 0.9999734386011124
BIAS_TWO = 0.09520785288629041

INV_PI = 0.3183098861837907


def turned(halves):
    return halves - jnp.round(halves)


def sine(u, z):
    p = 0.07764279097318649
    for c in (-0.5982846617698669, 2.550076723098755, -5.167709827423096, 3.1415927410125732):
        p = p * z + c
    return u * p


def double_cosine(z):
    p = -0.04924729838967323
    for c in (0.47014570236206055, -2.6704795360565186, 8.117423057556152, -9.869604110717773, 2.0):
        p = p * z + c
    return p


def unit_kernel(
    core_ref, x_hbm, cot_hbm, al_hbm, w_hbm, keep_ref, send_ref,
    x_ref, cot_ref, al_ref, flat_ref, wide_ref, w_ref, pad_ref, first_ref, second_ref, windows_ref, sems,
):
    frames = x_ref.shape[0]
    pairs = [(al_hbm, al_ref), (w_hbm, flat_ref), (cot_hbm, cot_ref)]
    for i in range(0, frames, CHUNK):
        pairs.insert(1 + i // CHUNK, (x_hbm.at[pl.ds(i, CHUNK)], x_ref.at[pl.ds(i, CHUNK)]))
    copies = [pltpu.make_async_copy(source, target, sems.at[n]) for n, (source, target) in enumerate(pairs)]
    for copy in copies:
        copy.start()
    rows = w_ref.shape[0]
    even = core_ref[0] == 0
    pad_ref[0:PAD, :] = jnp.zeros((PAD, CH), jnp.bfloat16)
    pad_ref[PAD + frames : 2 * PAD + frames, :] = jnp.zeros((PAD, CH), jnp.bfloat16)
    copies[0].wait()
    a0 = al_ref[0:1, :]
    a1 = al_ref[1:2, :]
    r0 = 1.0 / a0
    r1 = 1.0 / a1
    t0 = a0 * INV_PI
    t1 = a1 * INV_PI
    for i in range(0, frames, CHUNK):
        copies[1 + i // CHUNK].wait()
        x = x_ref[i : i + CHUNK, :].astype(jnp.float32)
        u = turned(t0 * x)
        s = sine(u, u * u)
        first = (x + s * s * r0).astype(jnp.bfloat16)
        first_ref[i : i + CHUNK, :] = first
        pad_ref[PAD + i : PAD + i + CHUNK, :] = first
    copies[-2].wait()
    wide_ref[...] = flat_ref[...].astype(jnp.float32)
    for side in range(2):
        half = wide_ref[pl.ds(side, rows, stride=2), :]
        w_ref[:, side * 128 : (side + 1) * 128] = half.astype(jnp.bfloat16)
    w_point = w_ref[TAPS * CH :, :]
    copies[-1].wait()
    for k in range(TAPS):
        off = PAD + DILATION * (k - TAPS // 2)
        windows_ref[:, k * CH : (k + 1) * CH] = pad_ref[off : off + frames, :]
    d_hidden = []
    for i in range(0, frames, CHUNK):
        hidden = jnp.dot(windows_ref[i : i + CHUNK, :], w_ref[: TAPS * CH, :], preferred_element_type=jnp.float32)
        u = turned(t1 * hidden)
        z = u * u
        s = sine(u, z)
        second_ref[i : i + CHUNK, :] = (hidden + s * s * r1).astype(jnp.bfloat16)
        back = lax.dot_general(
            cot_ref[i : i + CHUNK, :], w_point, (((1,), (1,)), ((), ())), preferred_element_type=jnp.float32
        )
        d_hidden.append((back * (1.0 + s * double_cosine(z))).astype(jnp.bfloat16))
    for n, i in enumerate(range(0, frames, CHUNK)):
        pad_ref[PAD + i : PAD + i + CHUNK, :] = d_hidden[n]
    for k in range(TAPS + 1):
        if k < TAPS:
            off = PAD - DILATION * (k - TAPS // 2)
            left, right = first_ref[...], pad_ref[off : off + frames, :]
        else:
            left, right = second_ref[...], cot_ref[...]
        grad = lax.dot_general(left, right, (((0,), (0,)), ((), ())), preferred_element_type=jnp.float32)
        for j in range(0, CH // BLOCK, 2):
            low = grad[j * BLOCK : (j + 1) * BLOCK, :]
            high = grad[(j + 1) * BLOCK : (j + 2) * BLOCK, :]
            slot = (k * (CH // BLOCK) + j) // 2
            keep_ref[slot] = jnp.where(even, low, high)
            send_ref[slot] = jnp.where(even, high, low)


def clip_grads(clip, cot, alphas, weights, core):
    frames = clip.shape[0]
    rows = (TAPS + 1) * CH
    vmem = pl.BlockSpec(memory_space=pltpu.VMEM)
    half = jax.ShapeDtypeStruct((32, BLOCK, CH), jnp.float32)
    return pl.pallas_call(
        unit_kernel,
        out_shape=(half, half),
        in_specs=[pl.BlockSpec(memory_space=pltpu.SMEM)] + [pl.BlockSpec(memory_space=pltpu.HBM)] * 4,
        out_specs=(vmem, vmem),
        scratch_shapes=[
            pltpu.VMEM((frames, CH), jnp.bfloat16),
            pltpu.VMEM((frames, CH), jnp.bfloat16),
            pltpu.VMEM((2, CH), jnp.float32),
            pltpu.VMEM((2 * rows, 128), jnp.bfloat16),
            pltpu.VMEM((2 * rows, 128), jnp.float32),
            pltpu.VMEM((rows, CH), jnp.bfloat16),
            pltpu.VMEM((frames + 2 * PAD, CH), jnp.bfloat16),
            pltpu.VMEM((frames, CH), jnp.bfloat16),
            pltpu.VMEM((frames, CH), jnp.bfloat16),
            pltpu.VMEM((frames, TAPS * CH), jnp.bfloat16),
            pltpu.SemaphoreType.DMA((3 + frames // CHUNK,)),
        ],
        compiler_params=pltpu.CompilerParams(vmem_limit_bytes=40 << 20),
        cost_estimate=pl.CostEstimate(flops=2200000000, bytes_accessed=5 << 20, transcendentals=0),
    )(core, *[pltpu.with_memory_space_constraint(v, pltpu.HBM) for v in (clip, cot, alphas, weights.reshape(2 * rows, 128))])


def first_half_kernel(core_ref, piece_ref, out_ref, sem):
    copy = pltpu.make_async_copy(piece_ref, out_ref.at[:, core_ref[0]], sem)
    copy.start()
    copy.wait()


def second_half_kernel(core_ref, piece_ref, begun_ref, out_ref, sem):
    copy = pltpu.make_async_copy(piece_ref, out_ref.at[:, 1 - core_ref[0]], sem)
    copy.start()
    copy.wait()


def place(kernel, core, piece, *begun):
    hbm = pl.BlockSpec(memory_space=pltpu.HBM)
    return pl.pallas_call(
        kernel,
        out_shape=jax.ShapeDtypeStruct((32, 2, 64, 128), jnp.bfloat16),
        in_specs=[pl.BlockSpec(memory_space=pltpu.SMEM), pl.BlockSpec(memory_space=pltpu.VMEM)] + [hbm] * len(begun),
        out_specs=hbm,
        scratch_shapes=[pltpu.SemaphoreType.DMA],
        input_output_aliases={2: 0} if begun else {},
        compiler_params=pltpu.CompilerParams(vmem_limit_bytes=4 << 20),
        cost_estimate=pl.CostEstimate(flops=0, bytes_accessed=1 << 20, transcendentals=0),
    )(core, piece, *begun)


def adam_update(gradient, master, first_part, second_part):
    new_first = first_part + 0.1 * gradient
    new_second = second_part + 0.001 * gradient * gradient
    new_master = master - 0.001 * (new_first / BIAS_ONE) / (jnp.sqrt(new_second / BIAS_TWO) + 1e-08)
    return (new_master, new_first, new_second)


SWAP = [(0, 1), (1, 0)]


def packed(values):
    return (values * lax.rsqrt(jnp.maximum(jnp.abs(values), 1e-30))).astype(jnp.float16)


def unpacked(roots):
    roots = roots.astype(jnp.float32)
    return roots * jnp.abs(roots)


def shards(clips, cotangent, alphas, weights, master, first_moment, second_moment):
    core = lax.axis_index("c").reshape(1)
    keep, send = clip_grads(clips[0], cotangent[0], alphas, weights, core)
    ready = jnp.concatenate([master, 0.9 * first_moment, 0.999 * second_moment])
    recv, ready = lax.optimization_barrier((lax.ppermute(send, "c", SWAP), ready))
    part = packed(keep + recv).reshape(128, QUARTER, CH)
    part = jnp.sum(unpacked(lax.all_to_all(part, ("zl", "y", "x"), 0, 0, tiled=True)), axis=0)
    part = jnp.broadcast_to(part[None], (16, QUARTER, CH))
    part = lax.all_to_all(part, ("zh", "x"), 0, 0, tiled=True)
    gradient = jnp.sum(part.reshape(4, BLOCK, CH), axis=0).reshape(-1)
    new_master, new_first, new_second = adam_update(gradient, *jnp.split(ready, 3))
    piece = new_master.astype(jnp.bfloat16).reshape(64, 128)
    piece = lax.all_to_all(jnp.broadcast_to(piece[None], (32, 64, 128)), ("zl", "y"), 0, 0, tiled=True)
    other = lax.ppermute(piece, "c", SWAP)
    half = place(first_half_kernel, core, piece)
    new_weights = place(second_half_kernel, core, other, half).reshape(-1)
    return (new_weights, new_master, new_first, new_second)


def solution(mesh):
    fine = Mesh(mesh.devices.reshape(4, 8, 2, 4, 4), ("zl", "y", "c", "zh", "x"))
    dp = ("zl", "y", "c")
    every = P(dp + ("zh", "x"), None, None)
    return jax.shard_map(
        shards,
        mesh=fine,
        in_specs=(every, every, P(), P(), P(dp), P(dp), P(dp)),
        out_specs=(P(), P(dp), P(dp), P(dp)),
        check_vma=False,
    )
```

```python
import jax
import jax.numpy as jnp
from jax import lax
from jax.experimental import pallas as pl
from jax.experimental.pallas import tpu as pltpu
from jax.sharding import Mesh, PartitionSpec as P

CH = 256
TAPS = 7
DILATION = 3
PAD = 16
CHUNK = 256
BLOCK = 32

BIAS_ONE = 0.9999734386011124
BIAS_TWO = 0.09520785288629041

INV_PI = 0.3183098861837907


def turned(halves):
    return halves - jnp.round(halves)


def sine(u, z):
    p = 0.07764279097318649
    for c in (-0.5982846617698669, 2.550076723098755, -5.167709827423096, 3.1415927410125732):
        p = p * z + c
    return u * p


def double_cosine(z):
    p = -0.04924729838967323
    for c in (0.47014570236206055, -2.6704795360565186, 8.117423057556152, -9.869604110717773, 2.0):
        p = p * z + c
    return p


def unit_kernel(
    core_ref, x_hbm, cot_hbm, al_hbm, w_hbm, keep_ref, send_ref,
    x_ref, cot_ref, al_ref, flat_ref, wide_ref, w_ref, pad_ref, first_ref, second_ref, windows_ref, sems,
):
    frames = x_ref.shape[0]
    pairs = [(al_hbm, al_ref), (w_hbm, flat_ref), (cot_hbm, cot_ref)]
    for i in range(0, frames, CHUNK):
        pairs.insert(1 + i // CHUNK, (x_hbm.at[pl.ds(i, CHUNK)], x_ref.at[pl.ds(i, CHUNK)]))
    copies = [pltpu.make_async_copy(source, target, sems.at[n]) for n, (source, target) in enumerate(pairs)]
    for copy in copies:
        copy.start()
    rows = w_ref.shape[0]
    even = core_ref[0] == 0
    pad_ref[0:PAD, :] = jnp.zeros((PAD, CH), jnp.bfloat16)
    pad_ref[PAD + frames : 2 * PAD + frames, :] = jnp.zeros((PAD, CH), jnp.bfloat16)
    copies[0].wait()
    a0 = al_ref[0:1, :]
    a1 = al_ref[1:2, :]
    r0 = 1.0 / a0
    r1 = 1.0 / a1
    t0 = a0 * INV_PI
    t1 = a1 * INV_PI
    for i in range(0, frames, CHUNK):
        copies[1 + i // CHUNK].wait()
        x = x_ref[i : i + CHUNK, :].astype(jnp.float32)
        u = turned(t0 * x)
        s = sine(u, u * u)
        first = (x + s * s * r0).astype(jnp.bfloat16)
        first_ref[i : i + CHUNK, :] = first
        pad_ref[PAD + i : PAD + i + CHUNK, :] = first
    copies[-2].wait()
    wide_ref[...] = flat_ref[...].astype(jnp.float32)
    for side in range(2):
        half = wide_ref[pl.ds(side, rows, stride=2), :]
        w_ref[:, side * 128 : (side + 1) * 128] = half.astype(jnp.bfloat16)
    w_point = w_ref[TAPS * CH :, :]
    copies[-1].wait()
    for k in range(TAPS):
        off = PAD + DILATION * (k - TAPS // 2)
        windows_ref[:, k * CH : (k + 1) * CH] = pad_ref[off : off + frames, :]
    d_hidden = []
    for i in range(0, frames, CHUNK):
        hidden = jnp.dot(windows_ref[i : i + CHUNK, :], w_ref[: TAPS * CH, :], preferred_element_type=jnp.float32)
        u = turned(t1 * hidden)
        z = u * u
        s = sine(u, z)
        second_ref[i : i + CHUNK, :] = (hidden + s * s * r1).astype(jnp.bfloat16)
        back = lax.dot_general(
            cot_ref[i : i + CHUNK, :], w_point, (((1,), (1,)), ((), ())), preferred_element_type=jnp.float32
        )
        d_hidden.append((back * (1.0 + s * double_cosine(z))).astype(jnp.bfloat16))
    for n, i in enumerate(range(0, frames, CHUNK)):
        pad_ref[PAD + i : PAD + i + CHUNK, :] = d_hidden[n]
    for k in range(TAPS + 1):
        if k < TAPS:
            off = PAD - DILATION * (k - TAPS // 2)
            left, right = first_ref[...], pad_ref[off : off + frames, :]
        else:
            left, right = second_ref[...], cot_ref[...]
        grad = lax.dot_general(left, right, (((0,), (0,)), ((), ())), preferred_element_type=jnp.float32)
        for j in range(0, CH // BLOCK, 2):
            low = grad[j * BLOCK : (j + 1) * BLOCK, :]
            high = grad[(j + 1) * BLOCK : (j + 2) * BLOCK, :]
            slot = (k * (CH // BLOCK) + j) // 2
            keep_ref[slot] = jnp.where(even, low, high)
            send_ref[slot] = jnp.where(even, high, low)


def clip_grads(clip, cot, alphas, weights, core):
    frames = clip.shape[0]
    rows = (TAPS + 1) * CH
    vmem = pl.BlockSpec(memory_space=pltpu.VMEM)
    half = jax.ShapeDtypeStruct((32, BLOCK, CH), jnp.float32)
    return pl.pallas_call(
        unit_kernel,
        out_shape=(half, half),
        in_specs=[pl.BlockSpec(memory_space=pltpu.SMEM)] + [pl.BlockSpec(memory_space=pltpu.HBM)] * 4,
        out_specs=(vmem, vmem),
        scratch_shapes=[
            pltpu.VMEM((frames, CH), jnp.bfloat16),
            pltpu.VMEM((frames, CH), jnp.bfloat16),
            pltpu.VMEM((2, CH), jnp.float32),
            pltpu.VMEM((2 * rows, 128), jnp.bfloat16),
            pltpu.VMEM((2 * rows, 128), jnp.float32),
            pltpu.VMEM((rows, CH), jnp.bfloat16),
            pltpu.VMEM((frames + 2 * PAD, CH), jnp.bfloat16),
            pltpu.VMEM((frames, CH), jnp.bfloat16),
            pltpu.VMEM((frames, CH), jnp.bfloat16),
            pltpu.VMEM((frames, TAPS * CH), jnp.bfloat16),
            pltpu.SemaphoreType.DMA((3 + frames // CHUNK,)),
        ],
        compiler_params=pltpu.CompilerParams(vmem_limit_bytes=40 << 20),
        cost_estimate=pl.CostEstimate(flops=2200000000, bytes_accessed=5 << 20, transcendentals=0),
    )(core, *[pltpu.with_memory_space_constraint(v, pltpu.HBM) for v in (clip, cot, alphas, weights.reshape(2 * rows, 128))])


def first_half_kernel(core_ref, piece_ref, out_ref, sem):
    copy = pltpu.make_async_copy(piece_ref, out_ref.at[:, core_ref[0]], sem)
    copy.start()
    copy.wait()


def second_half_kernel(core_ref, piece_ref, begun_ref, out_ref, sem):
    copy = pltpu.make_async_copy(piece_ref, out_ref.at[:, 1 - core_ref[0]], sem)
    copy.start()
    copy.wait()


def place(kernel, core, piece, *begun):
    hbm = pl.BlockSpec(memory_space=pltpu.HBM)
    return pl.pallas_call(
        kernel,
        out_shape=jax.ShapeDtypeStruct((32, 2, 64, 128), jnp.bfloat16),
        in_specs=[pl.BlockSpec(memory_space=pltpu.SMEM), pl.BlockSpec(memory_space=pltpu.VMEM)] + [hbm] * len(begun),
        out_specs=hbm,
        scratch_shapes=[pltpu.SemaphoreType.DMA],
        input_output_aliases={2: 0} if begun else {},
        compiler_params=pltpu.CompilerParams(vmem_limit_bytes=4 << 20),
        cost_estimate=pl.CostEstimate(flops=0, bytes_accessed=1 << 20, transcendentals=0),
    )(core, piece, *begun)


def adam_update(gradient, master, first_part, second_part):
    new_first = first_part + 0.1 * gradient
    new_second = second_part + 0.001 * gradient * gradient
    new_master = master - 0.001 * (new_first / BIAS_ONE) / (jnp.sqrt(new_second / BIAS_TWO) + 1e-08)
    return (new_master, new_first, new_second)


SWAP = [(0, 1), (1, 0)]


def packed(values):
    return (values * lax.rsqrt(jnp.maximum(jnp.abs(values), 1e-30))).astype(jnp.float16)


def unpacked(roots):
    roots = roots.astype(jnp.float32)
    return roots * jnp.abs(roots)


def shards(clips, cotangent, alphas, weights, master, first_moment, second_moment):
    core = lax.axis_index("c").reshape(1)
    keep, send = clip_grads(clips[0], cotangent[0], alphas, weights, core)
    ready = jnp.concatenate([master, 0.9 * first_moment, 0.999 * second_moment])
    recv, ready = lax.optimization_barrier((lax.ppermute(send, "c", SWAP), ready))
    part = lax.all_to_all(packed(keep + recv), ("zl", "y"), 0, 0, tiled=True)
    part = jnp.sum(unpacked(part), axis=0)
    for axis in ("x", "zh"):
        part = jnp.broadcast_to(part[None], (4, BLOCK, CH))
        part = jnp.sum(lax.all_to_all(part, axis, 0, 0, tiled=True), axis=0)
    gradient = part.reshape(-1)
    new_master, new_first, new_second = adam_update(gradient, *jnp.split(ready, 3))
    piece = new_master.astype(jnp.bfloat16).reshape(64, 128)
    piece = lax.all_to_all(jnp.broadcast_to(piece[None], (32, 64, 128)), ("zl", "y"), 0, 0, tiled=True)
    other = lax.ppermute(piece, "c", SWAP)
    half = place(first_half_kernel, core, piece)
    new_weights = place(second_half_kernel, core, other, half).reshape(-1)
    return (new_weights, new_master, new_first, new_second)


def solution(mesh):
    fine = Mesh(mesh.devices.reshape(4, 8, 2, 4, 4), ("zl", "y", "c", "zh", "x"))
    dp = ("zl", "y", "c")
    every = P(dp + ("zh", "x"), None, None)
    return jax.shard_map(
        shards,
        mesh=fine,
        in_specs=(every, every, P(), P(), P(dp), P(dp), P(dp)),
        out_specs=(P(), P(dp), P(dp), P(dp)),
        check_vma=False,
    )
```
